32 devices in a mesh: ia: 4 (over z), ja: 4 (over y, x), ka: 2 (over core).
Axes of the slice: x: 2, y: 2, z: 4, core: 2. Of those that a mesh axis runs over, the one named last changes fastest.
Arguments:
- blocks: bfloat16 [4, 4, 4, 128, 128, 128], P('ia', 'ja', 'ka'), may hold values from -6 to 6
- coordinates: int32 [3, 4, 4, 4], P(None, 'ia', 'ja', 'ka'), may hold values from 0 to 3, as said below
- occupancy: int32 [4, 4, 4], P('ia', 'ja', 'ka'), may hold values from 0 to 1, as said below
- second_factor: bfloat16 [4, 512, 1024], P('ja', ('ia', 'ka')), may hold values from -12 to 12
- third_factor: bfloat16 [2, 512, 1024], P('ka', ('ia', 'ja')), may hold values from -0.0234375 to 0.0234375
- inverse_first: bfloat16 [1024, 1024], replicated
- inverse_second: bfloat16 [1024, 1024], replicated
Outputs:
- first_new: bfloat16 [4, 512, 1024], P('ia', ('ja', 'ka'))
- second_new: bfloat16 [4, 512, 1024], P('ja', ('ia', 'ka'))
The draws below stay inside these ranges and needn't reach their ends.
Inputs may be any that keep to these rules, and one draw needn't show every extreme that they name: `occupancy`: each device has two slots; its second slot is occupied only where its first is. A device with two blocks is followed along ka, cyclically, by a device with none. Some device holds two blocks. coordinates[0], [1], [2] of a slot are a block row among 4, a block row among 4 and a block layer among 4 of its device's ranges; the two slots of a device name different layers.
All inputs are finite; a program needn't handle non-finite values.
Results may differ from the reference program's by a relative error of at most 0.006.
Values may be sent and summed in bfloat16 or wider, within the bound.
A program may use at most 128 MiB of HBM per device.

```python
import jax
import jax.numpy as jnp
from jax import lax

R = 1024
BLK = 128
SLOTS = 2
IB = 4
JB = 4
KB = 4
N_IA = 4
N_JA = 4
N_KA = 2


def draw_occupancy(key, part):
    subkeys = jax.random.split(jax.random.fold_in(key, 31), 3)
    cycles = N_IA * N_JA
    draws_raw = jax.random.randint(subkeys[0], (cycles, N_KA), 0, 20)
    counts = jnp.where(draws_raw < 7, 0, jnp.where(draws_raw < 14, 1, 2))
    forced_cycle = jax.random.randint(subkeys[1], (), 0, cycles)
    forced_place = jax.random.randint(subkeys[2], (), 0, N_KA)
    cycle_ids = jnp.arange(cycles)[:, None]
    positions = jnp.arange(N_KA)[None, :]
    counts = jnp.where((cycle_ids == forced_cycle) & (positions == forced_place), 2, counts)
    counts = jnp.where((cycle_ids == forced_cycle) & (positions == (forced_place + N_KA - 1) % N_KA), 0, counts)
    previous = jnp.roll(counts, 1, axis=1)
    counts = jnp.where(previous == 2, 0, counts)
    occupied = jnp.stack([counts >= 1, counts >= 2], axis=-1).astype(jnp.int32)
    return occupied.reshape(N_IA, N_JA, N_KA * SLOTS)


def draw_coordinates(key, part):
    subkeys = jax.random.split(jax.random.fold_in(key, 41), 4)
    shape_dev = (N_IA, N_JA, N_KA, SLOTS)
    first_rows = jax.random.randint(subkeys[0], shape_dev, 0, IB)
    second_rows = jax.random.randint(subkeys[1], shape_dev, 0, JB)
    layer_first = jax.random.randint(subkeys[2], (N_IA, N_JA, N_KA), 0, KB)
    layer_step = jax.random.randint(subkeys[3], (N_IA, N_JA, N_KA), 1, KB)
    layers = jnp.stack([layer_first, (layer_first + layer_step) % KB], axis=-1)
    stacked = jnp.stack([first_rows, second_rows, layers], axis=0)
    return stacked.reshape(3, N_IA, N_JA, N_KA * SLOTS).astype(jnp.int32)


def gram_inverse(noise, diag_key):
    diagonal = jax.random.uniform(diag_key, (R,), jnp.float32, 0.4, 1.0)
    symmetric = (noise + noise.T) * (0.2 / (2.0 * R) ** 0.5)
    on_diagonal = jnp.arange(R)[:, None] == jnp.arange(R)[None, :]
    return symmetric + jnp.where(on_diagonal, diagonal[None, :], 0.0)


def draw_inverse_first(key, part):
    subkeys = jax.random.split(jax.random.fold_in(key, 11), 2)
    noise = jax.random.normal(subkeys[0], (R, R), jnp.float32)
    return gram_inverse(noise, subkeys[1]).astype(jnp.bfloat16)


def draw_inverse_second(key, part):
    subkeys = jax.random.split(jax.random.fold_in(key, 12), 2)
    noise = jax.random.normal(subkeys[0], (R, R), jnp.float32)
    return gram_inverse(noise, subkeys[1]).astype(jnp.bfloat16)


def shard_levels(key, extent, pieces, least, largest):
    gain, own = 1.0, jax.random.fold_in(key, 6)
    for dim, shards_of in pieces:
        draws = jnp.exp(jax.random.uniform(jax.random.fold_in(own, dim), (shards_of,), jnp.float32, least / len(pieces), largest / len(pieces)))
        gain = gain * jnp.repeat(draws, extent[dim] // shards_of).reshape([-1 if axis == dim else 1 for axis in range(len(extent))])
    return gain


def gaussian(rng, extent, width, most, cuts=(), kind=jnp.bfloat16):
    drawn = width * jax.random.normal(rng, extent, jnp.float32)
    if cuts:
        drawn = drawn * shard_levels(rng, extent, cuts, -0.22, 0.18)
    return jnp.clip(drawn, -most, most).astype(kind)


def setup_inputs(seed: int = 0) -> dict:
    keys = jax.random.split(jax.random.key(seed), 8)
    return {
        "blocks": gaussian(keys[0], (N_IA, N_JA, N_KA * SLOTS, BLK, BLK, BLK), 1.0, 6.0, ((0, 4), (1, 4), (2, 2))),
        "coordinates": draw_coordinates(jax.random.fold_in(keys[7], 71), 0),
        "occupancy": draw_occupancy(jax.random.fold_in(keys[7], 71), 0),
        "second_factor": gaussian(keys[3], (N_JA, JB * BLK, R), 2.0, 12.0, ((0, 4), (1, 8))),
        "third_factor": gaussian(keys[4], (N_KA, KB * BLK, R), 0.004, 0.0234375, ((0, 2), (1, 16))),
        "inverse_first": draw_inverse_first(jax.random.fold_in(keys[7], 71), 0),
        "inverse_second": draw_inverse_second(jax.random.fold_in(keys[7], 71), 0),
    }


def reference(blocks, coordinates, occupancy, second_factor, third_factor, inverse_first, inverse_second):
    total_slots = N_IA * N_JA * N_KA * SLOTS
    flat_blocks = blocks.reshape(total_slots, BLK, BLK, BLK)
    places = coordinates.reshape(3, total_slots)
    occupied = occupancy.reshape(total_slots)
    slot_ids = jnp.arange(total_slots, dtype=jnp.int32)
    first_plane = slot_ids // (N_JA * N_KA * SLOTS)
    second_plane = (slot_ids // (N_KA * SLOTS)) % N_JA
    third_plane = (slot_ids // SLOTS) % N_KA
    row_block = (first_plane * IB + places[0]).astype(jnp.int32)
    col_block = (second_plane * JB + places[1]).astype(jnp.int32)
    layer_block = (third_plane * KB + places[2]).astype(jnp.int32)
    second_table = second_factor.reshape(N_JA * JB * BLK, R)
    third_table = third_factor.reshape(N_KA * KB * BLK, R)

    def mode_sum(target_rows, own_block, left_block, left_table, swapped):
        def add_block(totals, slot_index):
            def include(carry):
                tensor_block = lax.dynamic_index_in_dim(flat_blocks, slot_index, 0, keepdims=False)
                if swapped:
                    tensor_block = jnp.transpose(tensor_block, (1, 0, 2))
                left_slab = lax.dynamic_slice_in_dim(left_table, left_block[slot_index] * BLK, BLK, 0)
                layer_slab = lax.dynamic_slice_in_dim(third_table, layer_block[slot_index] * BLK, BLK, 0)
                khatri = (left_slab[:, None, :].astype(jnp.float32) * layer_slab[None, :, :].astype(jnp.float32)).astype(jnp.bfloat16)
                product = jnp.dot(tensor_block.reshape(BLK, BLK * BLK), khatri.reshape(BLK * BLK, R), preferred_element_type=jnp.float32)
                row_start = own_block[slot_index] * BLK
                current = lax.dynamic_slice_in_dim(carry, row_start, BLK, 0)
                return lax.dynamic_update_slice_in_dim(carry, current + product, row_start, 0)
            return lax.cond(occupied[slot_index] > 0, include, lambda carry: carry, totals), None
        zeroed = jnp.zeros((target_rows, R), jnp.float32)
        result, unused = lax.scan(add_block, zeroed, slot_ids)
        return result

    first_sum = mode_sum(N_IA * IB * BLK, row_block, col_block, second_table, False)
    first_new = jnp.dot(first_sum.astype(jnp.bfloat16), inverse_first, preferred_element_type=jnp.float32).astype(jnp.bfloat16)
    second_sum = mode_sum(N_JA * JB * BLK, col_block, row_block, first_new, True)
    second_new = jnp.dot(second_sum.astype(jnp.bfloat16), inverse_second, preferred_element_type=jnp.float32).astype(jnp.bfloat16)
    return first_new.reshape(N_IA, IB * BLK, R), second_new.reshape(N_JA, JB * BLK, R)
```

```python
import functools

import jax
import jax.numpy as jnp
from jax import lax
from jax.experimental import pallas as pl
from jax.experimental.pallas import tpu as pltpu
from jax.sharding import PartitionSpec as P

IB = 4
JB = 4
TILES = 4
GROUP = 32
MESH = pl.DeviceIdType.MESH
AXES = ("ia", "ja", "ka")


def kernel(
    sizes,
    blocks,
    places_in,
    occupied_in,
    second_in,
    third_in,
    inverse_first,
    inverse_second,
    first_out,
    second_out,
    xbuf,
    inv1,
    inv2,
    meta_s,
    meta_r,
    cbuf,
    bbuf,
    slab_s,
    slab_r,
    cuse,
    buse,
    tbuf,
    oacc,
    d1s,
    d1r,
    keep1,
    p1s,
    p1r,
    own1,
    total1,
    abuf,
    d2s,
    d2r,
    keep2,
    p2s,
    p2r,
    own2,
    total2,
    obuf,
    places,
    occupied,
    local_sem,
    once_send,
    once_recv,
    send_sem,
    recv_sem,
):
    na, nb, nc = sizes
    tiles, edge, width = slab_s.shape
    rs, rt = bbuf.shape[3], cbuf.shape[3]
    sh1, sh2 = abuf.shape[3], own2.shape[1]
    a, b, c = (lax.axis_index(name) for name in AXES)
    def away(axis, d):
        n = sizes[AXES.index(axis)]
        me = (a, b, c)[AXES.index(axis)]
        return lax.rem(me + d, n)

    def send(src, dst, send_sem, recv_sem, axis, d):
        copy = pltpu.make_async_remote_copy(
            src_ref=src,
            dst_ref=dst,
            send_sem=send_sem,
            recv_sem=recv_sem,
            device_id={axis: away(axis, d)},
            device_id_type=MESH,
        )
        copy.start()

    barrier = pltpu.get_barrier_semaphore()
    for axis, n in zip(AXES, sizes):
        for d in range(1, n):
            pl.semaphore_signal(
                barrier, inc=1, device_id={axis: away(axis, d)}, device_id_type=MESH
            )
    def cols(t):
        return pl.ds(t * width, width)

    def landed(ref, sem):
        pltpu.make_async_copy(ref, ref, sem).wait()

    def local_copy(src, dst, n):
        pltpu.make_async_copy(src, dst, local_sem.at[n]).start()

    local_copy(places_in, places, 0)
    local_copy(occupied_in, occupied, 1)
    for t in range(tiles):
        local_copy(third_in.at[0, :, cols(t)], cbuf.at[t, a, b], 2)
        local_copy(second_in.at[0, :, cols(t)], bbuf.at[t, a, c], 3)
    local_copy(blocks.at[0, 0, 0], xbuf.at[0], 4)
    local_copy(inverse_first, inv1, 5)
    local_copy(inverse_second, inv2, 6)
    landed(places, local_sem.at[0])
    landed(occupied, local_sem.at[1])
    keep = occupied[0, 0, 0] > 0
    row0, col0, layer0 = (places[0, 0, 0, m] for m in range(3))
    row1, col1, layer1 = (places[0, 0, 1, m] for m in range(3))
    weight1 = jnp.where(occupied[0, 0, 1] > 0, 1.0, 0.0).astype(jnp.float32)
    for q in range(IB):
        value = jnp.where(row1 == q, weight1, 0.0)
        meta_s[pl.ds(q, 1), :] = jnp.full((1, width), value, jnp.float32)
    for q in range(JB):
        value = jnp.where(col1 == q, weight1, 0.0)
        meta_s[pl.ds(IB + q, 1), :] = jnp.full((1, width), value, jnp.float32)
    pl.semaphore_wait(barrier, (na - 1) + (nb - 1) + (nc - 1))

    def chosen(own_value, row):
        own = jnp.where(own_value, 1.0, 0.0).astype(jnp.float32)
        return jnp.where(keep, jnp.full((1, width), own, jnp.float32), meta_r[pl.ds(row, 1), :]) > 0.5

    def third_column(t):
        for d in range(1, na):
            send(
                third_in.at[0, :, cols(t)],
                cbuf.at[t, a, b],
                send_sem.at[0],
                recv_sem.at[0, t],
                "ia",
                d,
            )

    def second_column(t):
        for d in range(1, na):
            send(
                second_in.at[0, :, cols(t)],
                bbuf.at[t, a, c],
                send_sem.at[1],
                recv_sem.at[1, t],
                "ia",
                d,
            )

    third_column(0)
    send(blocks.at[0, 0, 1], xbuf.at[1], once_send.at[0], once_recv.at[0], "ka", 1)
    send(meta_s, meta_r, once_send.at[1], once_recv.at[1], "ka", 1)
    for t in range(1, tiles):
        third_column(t)
        second_column(t - 1)
    second_column(tiles - 1)

    def spread_third(t):
        if t == 0:
            landed(cbuf.at[:, a, b], local_sem.at[2])
        landed(cbuf.at[t, pl.ds(0, na - 1), b], recv_sem.at[0, t])
        for d in range(1, nb):
            send(
                cbuf.at[t, :, b],
                cbuf.at[t, :, b],
                send_sem.at[2],
                recv_sem.at[2, t],
                "ja",
                d,
            )

    def spread_second(t):
        if t == 0:
            landed(bbuf.at[:, a, c], local_sem.at[3])
        landed(bbuf.at[t, pl.ds(0, na - 1), c], recv_sem.at[1, t])
        for d in range(1, nc):
            send(
                bbuf.at[t, :, c],
                bbuf.at[t, :, c],
                send_sem.at[3],
                recv_sem.at[3, t],
                "ka",
                d,
            )

    def layer_piece(t, layer, piece):
        per = edge // rt
        total = na * nb * rt // edge
        value = None
        for q in range(total):
            s = q * per + piece
            rows = cbuf[t, s // nb, s % nb]
            value = rows if value is None else jnp.where(layer == q, rows, value)
        return value

    def pass_slab(t):
        landed(cbuf.at[t, :, pl.ds(0, nb - 1)], recv_sem.at[2, t])
        for piece in range(edge // rt):
            slab_s[t, pl.ds(piece * rt, rt), :] = layer_piece(t, layer1, piece)
        send(slab_s.at[t], slab_r.at[t], send_sem.at[4], recv_sem.at[4, t], "ka", 1)

    def first_products(t, between):
        for piece in range(edge // rt):
            cuse[pl.ds(piece * rt, rt), :] = layer_piece(t, layer0, piece)
        landed(bbuf.at[t, :, pl.ds(0, nc - 1)], recv_sem.at[3, t])
        if t == 0:
            landed(xbuf.at[0], local_sem.at[4])
            landed(xbuf.at[1], once_recv.at[0])
            landed(meta_r, once_recv.at[1])
        masks = [chosen(col0 == q, IB + q) for q in range(JB)]
        per = edge // rs
        for piece in range(per):
            value = jnp.zeros((rs, width), jnp.float32)
            for q in range(JB):
                s = q * per + piece
                rows = bbuf[t, s // nc, s % nc].astype(jnp.float32)
                value = jnp.where(masks[q], rows, value)
            buse[pl.ds(piece * rs, rs), :] = value
        landed(slab_r.at[t], recv_sem.at[4, t])
        cuse[...] = jnp.where(keep, cuse[...], slab_r[t])
        slot = jnp.where(keep, 0, 1)

        def several(step, carry):
            base = pl.multiple_of(step * GROUP, GROUP)
            left = xbuf[slot, pl.ds(base, GROUP)].reshape(GROUP * edge, edge)
            product = jnp.dot(left, cuse[...], preferred_element_type=jnp.float32)
            sums = []
            for u in range(GROUP):
                part = product[u * edge : (u + 1) * edge]
                tbuf[t, base + u] = part.astype(jnp.bfloat16)
                sums.append(jnp.sum(part * buse[...], axis=0, keepdims=True))
            oacc[pl.ds(base, GROUP), :] = jnp.concatenate(sums, axis=0)
            return carry

        steps = edge // GROUP
        lax.fori_loop(0, steps // 2, several, 0)
        between()
        lax.fori_loop(steps // 2, steps, several, 0)

    def owned_piece(owner, rows, own_place, meta_row):
        start = owner * rows
        block = start // edge
        off = pl.multiple_of(start % edge, rows)
        mask = chosen(own_place == block, meta_row + block)
        return jnp.where(mask, oacc[pl.ds(off, rows), :], 0.0)

    def pair_sums(t, n, rows, own_place, meta_row, outgoing, arriving, kept, kind):
        for d in range(1, nc):
            for m in range(n):
                owner = m * nc + away("ka", d)
                outgoing[t, d - 1, m] = owned_piece(owner, rows, own_place, meta_row).astype(
                    jnp.bfloat16
                )
            send(
                outgoing.at[t, d - 1],
                arriving.at[t, d - 1],
                send_sem.at[kind],
                recv_sem.at[kind, t],
                "ka",
                d,
            )
        for m in range(n):
            kept[t, m] = owned_piece(m * nc + c, rows, own_place, meta_row)

    def chip_sums(t, axis, n, arriving, kept, outgoing, landing, own, pair, kind):
        landed(arriving.at[t], recv_sem.at[pair, t])
        for d in range(n):
            m = away(axis, d)
            value = kept[t, m]
            for e in range(1, nc):
                value = value + arriving[t, e - 1, m].astype(jnp.float32)
            if d == 0:
                own[t] = value
            else:
                outgoing[t, d - 1] = value.astype(jnp.bfloat16)
                send(
                    outgoing.at[t, d - 1],
                    landing.at[t, d - 1],
                    send_sem.at[kind],
                    recv_sem.at[kind, t],
                    axis,
                    d,
                )

    def first_chip_sums(t):
        chip_sums(t, "ja", nb, d1r, keep1, p1s, p1r, own1, 5, 6)

    def gathered(t, own, landing, n, kind):
        landed(landing.at[t], recv_sem.at[kind, t])
        value = own[t]
        for d in range(1, n):
            value = value + landing[t, d - 1].astype(jnp.float32)
        return value.astype(jnp.bfloat16)

    def fold(t, value, inverse, total):
        part = jnp.dot(value, inverse[cols(t), :], preferred_element_type=jnp.float32)
        total[...] = part if t == 0 else total[...] + part

    def first_fold(t):
        fold(t, gathered(t, own1, p1r, nb, 6), inv1, total1)

    spread_third(0)
    if tiles > 1:
        spread_third(1)
    spread_second(0)
    pass_slab(0)
    for t in range(tiles):

        def between(t=t):
            if t + 1 < tiles:
                spread_second(t + 1)
                pass_slab(t + 1)
            if t:
                first_chip_sums(t - 1)

        first_products(t, between)
        pair_sums(t, nb, sh1, row0, 0, d1s, d1r, keep1, 5)
        if t + 2 < tiles:
            spread_third(t + 2)
        if t == 1:
            landed(inv1, local_sem.at[5])
        if t > 1:
            first_fold(t - 2)
    first_chip_sums(tiles - 1)
    for t in range(max(tiles - 2, 0), tiles):
        first_fold(t)
    for t in range(tiles):
        abuf[t, b, c] = total1[:, cols(t)].astype(jnp.bfloat16)
        for d in range(1, nb):
            send(
                abuf.at[t, b, c],
                abuf.at[t, b, c],
                send_sem.at[7],
                recv_sem.at[7, t],
                "ja",
                d,
            )
    for t in range(tiles):
        local_copy(abuf.at[t, b, c], first_out.at[0, :, cols(t)], 7)

    def spread_new(t):
        landed(abuf.at[t, pl.ds(0, nb - 1), c], recv_sem.at[7, t])
        for d in range(1, nc):
            send(
                abuf.at[t, :, c],
                abuf.at[t, :, c],
                send_sem.at[8],
                recv_sem.at[8, t],
                "ka",
                d,
            )

    def second_products(t):
        landed(abuf.at[t, :, pl.ds(0, nc - 1)], recv_sem.at[8, t])
        masks = [chosen(row0 == q, q) for q in range(IB)]
        per = edge // sh1
        for piece in range(per):
            value = jnp.zeros((sh1, width), jnp.float32)
            for q in range(IB):
                s = q * per + piece
                rows = abuf[t, s // nc, s % nc].astype(jnp.float32)
                value = jnp.where(masks[q], rows, value)
            buse[pl.ds(piece * sh1, sh1), :] = value
        lanes = 128
        for lane in range(0, width, lanes):

            def eight(step, total):
                base = pl.multiple_of(step * 8, 8)
                rows = buse[pl.ds(base, 8), pl.ds(lane, lanes)]
                for u in range(8):
                    total = total + rows[u : u + 1] * tbuf[t, base + u, :, pl.ds(lane, lanes)].astype(
                        jnp.float32
                    )
                return total

            oacc[:, pl.ds(lane, lanes)] = lax.fori_loop(
                0, edge // 8, eight, jnp.zeros((edge, lanes), jnp.float32)
            )

    def second_chip_sums(t):
        chip_sums(t, "ia", na, d2r, keep2, p2s, p2r, own2, 9, 10)

    def second_fold(t):
        fold(t, gathered(t, own2, p2r, na, 10), inv2, total2)

    spread_new(0)
    for t in range(tiles):
        if t + 1 < tiles:
            spread_new(t + 1)
        second_products(t)
        pair_sums(t, na, sh2, col0, IB, d2s, d2r, keep2, 9)
        if t:
            second_chip_sums(t - 1)
        if t == 1:
            landed(inv2, local_sem.at[6])
        if t > 1:
            second_fold(t - 2)
    second_chip_sums(tiles - 1)
    for t in range(max(tiles - 2, 0), tiles):
        second_fold(t)
    obuf[...] = total2[...].astype(jnp.bfloat16)
    local_copy(obuf, second_out.at[0], 8)
    landed(blocks.at[0, 0, 1], once_send.at[0])
    landed(meta_s, once_send.at[1])
    landed(cbuf.at[:, pl.ds(0, na - 1), b], send_sem.at[0])
    landed(bbuf.at[:, pl.ds(0, na - 1), c], send_sem.at[1])
    landed(cbuf.at[:, :, pl.ds(0, nb - 1)], send_sem.at[2])
    landed(bbuf.at[:, :, pl.ds(0, nc - 1)], send_sem.at[3])
    landed(slab_s, send_sem.at[4])
    landed(d1s, send_sem.at[5])
    landed(p1s, send_sem.at[6])
    landed(abuf.at[:, pl.ds(0, nb - 1), c], send_sem.at[7])
    landed(abuf.at[:, :, pl.ds(0, nc - 1)], send_sem.at[8])
    landed(d2s, send_sem.at[9])
    landed(p2s, send_sem.at[10])
    landed(first_out.at[0], local_sem.at[7])
    landed(second_out.at[0], local_sem.at[8])


def body(
    sizes,
    blocks,
    coordinates,
    occupancy,
    second_factor,
    third_factor,
    inverse_first,
    inverse_second,
):
    coordinates = jnp.transpose(coordinates, (1, 2, 3, 0))
    na, nb, nc = sizes
    edge, rank = blocks.shape[-1], inverse_first.shape[0]
    tiles = TILES
    width = rank // tiles
    rs, rt = second_factor.shape[1], third_factor.shape[1]
    sh1, sh2 = IB * edge // (nb * nc), JB * edge // (na * nc)
    bf16, f32 = jnp.bfloat16, jnp.float32
    dma = pltpu.SemaphoreType.DMA
    vmem = pl.BlockSpec(memory_space=pltpu.VMEM)
    anywhere = pl.BlockSpec(memory_space=pl.ANY)
    scratch = [
        pltpu.VMEM((2, edge, edge, edge), bf16),
        pltpu.VMEM((rank, rank), bf16),
        pltpu.VMEM((rank, rank), bf16),
        pltpu.VMEM((IB + JB, width), f32),
        pltpu.VMEM((IB + JB, width), f32),
        pltpu.VMEM((tiles, na, nb, rt, width), bf16),
        pltpu.VMEM((tiles, na, nc, rs, width), bf16),
        pltpu.VMEM((tiles, edge, width), bf16),
        pltpu.VMEM((tiles, edge, width), bf16),
        pltpu.VMEM((edge, width), bf16),
        pltpu.VMEM((edge, width), f32),
        pltpu.VMEM((tiles, edge, edge, width), bf16),
        pltpu.VMEM((edge, width), f32),
        pltpu.VMEM((tiles, nc - 1, nb, sh1, width), bf16),
        pltpu.VMEM((tiles, nc - 1, nb, sh1, width), bf16),
        pltpu.VMEM((tiles, nb, sh1, width), f32),
        pltpu.VMEM((tiles, nb - 1, sh1, width), bf16),
        pltpu.VMEM((tiles, nb - 1, sh1, width), bf16),
        pltpu.VMEM((tiles, sh1, width), f32),
        pltpu.VMEM((sh1, rank), f32),
        pltpu.VMEM((tiles, nb, nc, sh1, width), bf16),
        pltpu.VMEM((tiles, nc - 1, na, sh2, width), bf16),
        pltpu.VMEM((tiles, nc - 1, na, sh2, width), bf16),
        pltpu.VMEM((tiles, na, sh2, width), f32),
        pltpu.VMEM((tiles, na - 1, sh2, width), bf16),
        pltpu.VMEM((tiles, na - 1, sh2, width), bf16),
        pltpu.VMEM((tiles, sh2, width), f32),
        pltpu.VMEM((sh2, rank), f32),
        pltpu.VMEM((sh2, rank), bf16),
        pltpu.SMEM(coordinates.shape, jnp.int32),
        pltpu.SMEM(occupancy.shape, jnp.int32),
        dma((9,)),
        dma((2,)),
        dma((2,)),
        dma((11,)),
        dma((11, tiles)),
    ]
    results = pl.pallas_call(
        functools.partial(kernel, sizes),
        name="als",
        out_shape=(
            jax.ShapeDtypeStruct((1, sh1, rank), bf16),
            jax.ShapeDtypeStruct((1, sh2, rank), bf16),
        ),
        in_specs=[anywhere, anywhere, anywhere, vmem, vmem, anywhere, anywhere],
        out_specs=(anywhere, anywhere),
        scratch_shapes=scratch,
        compiler_params=pltpu.CompilerParams(
            collective_id=0, has_side_effects=True, vmem_limit_bytes=67043328
        ),
    )(blocks, coordinates, occupancy, second_factor, third_factor, inverse_first, inverse_second)
    return pl.pallas_call(
        hand_over,
        name="hand_over",
        out_shape=tuple(jax.ShapeDtypeStruct(x.shape, x.dtype) for x in results),
        in_specs=[vmem, vmem],
        out_specs=(vmem, vmem),
    )(*results)


def hand_over(first_in, second_in, first_out, second_out):
    first_out[...] = first_in[...]
    second_out[...] = second_in[...]


def solution(mesh):
    sizes = tuple(mesh.shape[name] for name in AXES)
    in_specs = (
        P("ia", "ja", "ka", None, None, None),
        P(None, "ia", "ja", "ka"),
        P("ia", "ja", "ka"),
        P("ja", ("ia", "ka"), None),
        P("ka", ("ia", "ja"), None),
        P(),
        P(),
    )
    out_specs = (P("ia", ("ja", "ka"), None), P("ja", ("ia", "ka"), None))
    return jax.shard_map(
        functools.partial(body, sizes),
        mesh=mesh,
        in_specs=in_specs,
        out_specs=out_specs,
        check_vma=False,
    )
```
